32 devices in a mesh: dp: 8 (over z, x), sub: 4 (over y, core).
Axes of the slice: x: 2, y: 2, z: 4, core: 2. Of those that a mesh axis runs over, the one named last changes fastest.
Arguments:
- queries: bfloat16 [1024, 4096], P('dp', 'sub'), may hold values from -1 to 1
- passages: bfloat16 [48, 4096], P('dp', 'sub'), may hold values from -1 to 1
- positive_bank: bfloat16 [2048, 4096], P('dp', 'sub'), may hold values from -1 to 1
- positive_ids: int32 [1024, 16], P('dp'), may hold values from -1 to 2047, as said below
- positive_counts: int32 [1024], P('dp'), may hold values from 1 to 16
Outputs:
- losses: float32 [1024], P('dp')
- query_grad: float32 [1024, 4096], P('dp', 'sub')
- passage_grad: float32 [48, 4096], P('dp', 'sub')
- bank_grad: float32 [2048, 4096], P('dp', 'sub')
The draws below stay inside these ranges and needn't reach their ends.
Inputs may be any that keep to these rules, and one draw needn't show every extreme that they name: `positive_ids`: entries of row i before position positive_counts[i] are rows of positive_bank, the rest are -1. The valid entries of the 128 queries of one index of dp name rows held by any one index of dp at most 32 times in all (repeats counted), a bound that is reached. In each aligned block of 16 queries at most one query has more than one valid entry.
All inputs are finite; a program needn't handle non-finite values.
Results may differ from the reference program's by a relative error of at most 0.0019.
Values may be sent and summed in bfloat16 or wider, within the bound.
No kernel may reach another device: no remote copies, remote signals or barrier semaphores. Data moves between devices by JAX's collectives and lax.ppermute only.
A program may use at most 64 MiB of HBM per device.

```python
import jax
import jax.numpy as jnp
from jax import lax

D = 4096
Q_DEV = 128
MAXPOS = 16
CAP = 32
BANK_DEV = 256
Q_TOT = 1024
P_TOT = 48
B_TOT = 2048


def joint_embed(key):
    keys = jax.random.split(jax.random.fold_in(key, 11), 2)
    spread = (2500.0 * D) ** (-0.25)
    query_draw = jax.random.normal(keys[0], (Q_TOT, D), jnp.float32) * spread
    passage_draw = jax.random.normal(keys[1], (P_TOT, D), jnp.float32) * spread
    return (jnp.clip(query_draw, -1.0, 1.0), jnp.clip(passage_draw, -1.0, 1.0))


def draw_queries(key, part):
    return joint_embed(key)[0].astype(jnp.bfloat16)


def draw_passages(key, part):
    return joint_embed(key)[1].astype(jnp.bfloat16)


def draw_positive_bank(key, part):
    keys = jax.random.split(jax.random.fold_in(key, 31), 1)
    spread = (2500.0 * D) ** (-0.25)
    bank_draw = jax.random.normal(keys[0], (B_TOT, D), jnp.float32) * spread
    return jnp.clip(bank_draw, -1.0, 1.0).astype(jnp.bfloat16)


def request_plan(key):
    keys = jax.random.split(jax.random.fold_in(key, 23), 8)
    dev_count = Q_TOT // Q_DEV
    unit_count = dev_count * CAP
    block_count = Q_DEV // 16
    is_heavy = jax.random.randint(keys[0], (dev_count, 1), 0, 2)
    big_slot = jax.random.randint(keys[1], (dev_count, block_count), 0, 16)
    heavy_count = jax.random.randint(keys[2], (dev_count, block_count), 1, MAXPOS + 1)
    light_count = jax.random.randint(keys[3], (dev_count, block_count), 1, 5)
    big_count = jnp.where(is_heavy == 1, heavy_count, light_count)
    forced_dev = jax.random.randint(keys[4], (), 0, dev_count)
    forced_block = jax.random.randint(keys[5], (), 0, block_count)
    big_count = big_count.at[forced_dev, forced_block].set(MAXPOS)
    counts = jnp.where(jnp.arange(16)[None, None, :] == big_slot[:, :, None], big_count[:, :, None], 1)
    counts = counts.reshape(dev_count, Q_DEV).astype(jnp.int32)
    hot_owner = jax.random.randint(keys[6], (), 0, dev_count)

    def per_device(dev_key, dev_counts):
        sub_keys = jax.random.split(dev_key, 3)
        is_live = (jnp.arange(MAXPOS)[None, :] < dev_counts[:, None]).reshape(-1)
        live_rank = jnp.cumsum(is_live.astype(jnp.int32)) - 1
        hot_places = jax.random.permutation(sub_keys[0], Q_DEV)[:CAP]
        is_hot = jnp.zeros((unit_count,), jnp.int32).at[hot_places].set(1)
        hot_before = jnp.cumsum(is_hot) - is_hot
        cold_order = jax.random.permutation(sub_keys[1], unit_count - CAP)
        cold_unit = cold_order[jnp.clip(jnp.arange(unit_count) - hot_before, 0, unit_count - CAP - 1)]
        cold_unit = cold_unit + CAP * (cold_unit >= hot_owner * CAP).astype(jnp.int32)
        hot_unit = hot_owner * CAP + jnp.clip(hot_before, 0, CAP - 1)
        sequence = jnp.where(is_hot == 1, hot_unit, cold_unit)
        unit_of = sequence[jnp.clip(live_rank, 0, unit_count - 1)]
        local_row = jax.random.randint(sub_keys[2], (Q_DEV * MAXPOS,), 0, BANK_DEV)
        id_rows = jnp.where(is_live, unit_of // CAP * BANK_DEV + local_row, -1)
        return id_rows.reshape(Q_DEV, MAXPOS).astype(jnp.int32)
    id_table = jax.vmap(per_device)(jax.random.split(keys[7], dev_count), counts)
    return (id_table.reshape(Q_TOT, MAXPOS), counts.reshape(Q_TOT))


def draw_positive_ids(key, part):
    return request_plan(key)[0]


def draw_positive_counts(key, part):
    return request_plan(key)[1]


def setup_inputs(seed: int = 0) -> dict:
    arg_keys = jax.random.split(jax.random.key(seed), 6)
    return {
        "queries": draw_queries(jax.random.fold_in(arg_keys[5], 71), 0),
        "passages": draw_passages(jax.random.fold_in(arg_keys[5], 71), 0),
        "positive_bank": draw_positive_bank(jax.random.fold_in(arg_keys[5], 71), 0),
        "positive_ids": draw_positive_ids(jax.random.fold_in(arg_keys[5], 71), 0),
        "positive_counts": draw_positive_counts(jax.random.fold_in(arg_keys[5], 71), 0),
    }


def reference(queries, passages, positive_bank, positive_ids, positive_counts):
    query_total, col_width = queries.shape
    bank_total = positive_bank.shape[0]
    block_rows = 1024 if query_total % 1024 == 0 else query_total
    nblocks = query_total // block_rows
    query_blocks = queries.reshape(nblocks, block_rows, col_width)
    id_blocks = positive_ids.reshape(nblocks, block_rows, MAXPOS)
    count_blocks = positive_counts.reshape(nblocks, block_rows)
    slots = jnp.arange(MAXPOS, dtype=jnp.int32)

    def accumulate(running, block_item):
        passage_sum, bank_sum = running
        block_queries, block_ids, counts = block_item
        scores = jnp.dot(block_queries, passages.T, preferred_element_type=jnp.float32) * 50.0
        is_valid = slots[None, :] < counts[:, None]
        safe_ids = jnp.clip(block_ids, 0, bank_total - 1).astype(jnp.int32)
        fetched = positive_bank[safe_ids].astype(jnp.float32)
        query_f32 = block_queries.astype(jnp.float32)
        pos_scores = jnp.einsum("kd,kpd->kp", query_f32, fetched) * 50.0
        row_max = jnp.maximum(jnp.max(scores, 1), jnp.max(jnp.where(is_valid, pos_scores, -jnp.inf), 1))
        row_total = jnp.sum(jnp.exp(scores - row_max[:, None]), 1)
        row_total = row_total + jnp.sum(jnp.exp(jnp.where(is_valid, pos_scores - row_max[:, None], -jnp.inf)), 1)
        log_total = row_max + jnp.log(row_total)
        inv_count = 1.0 / counts.astype(jnp.float32)
        query_loss = log_total - jnp.sum(jnp.where(is_valid, pos_scores, 0.0), 1) * inv_count
        weights = jnp.exp(scores - log_total[:, None]).astype(jnp.bfloat16)
        coeffs = jnp.where(is_valid, jnp.exp(jnp.where(is_valid, pos_scores - log_total[:, None], -jnp.inf)) - inv_count[:, None], 0.0)
        query_grad = 50.0 * (jnp.dot(weights, passages, preferred_element_type=jnp.float32) + jnp.einsum("kp,kpd->kd", coeffs, fetched))
        passage_sum = passage_sum + jnp.dot(weights.T, block_queries, preferred_element_type=jnp.float32)
        segment_ids = jnp.where(is_valid, safe_ids, bank_total).reshape(-1)
        contrib = (coeffs[:, :, None] * query_f32[:, None, :]).reshape(-1, col_width)
        bank_sum = bank_sum + jax.ops.segment_sum(contrib, segment_ids, bank_total + 1)[:bank_total]
        return (passage_sum, bank_sum), (query_loss, query_grad)

    start_state = (jnp.zeros((passages.shape[0], col_width), jnp.float32), jnp.zeros((bank_total, col_width), jnp.float32))
    (passage_sum, bank_sum), (loss_blocks, grad_blocks) = lax.scan(accumulate, start_state, (query_blocks, id_blocks, count_blocks))
    losses = loss_blocks.reshape(query_total)
    query_grad = grad_blocks.reshape(query_total, col_width)
    return (losses, query_grad, 50.0 * passage_sum, 50.0 * bank_sum)
```

```python
import jax
import jax.numpy as jnp
from jax import lax
from jax.sharding import PartitionSpec as P

BF = jnp.bfloat16
F32 = jnp.float32


def exchange(x):
    return lax.all_to_all(x, "dp", split_axis=0, concat_axis=0, tiled=True)


def sub_sum(x):
    size = lax.axis_size("sub")
    step = 1
    while step < size:
        x = x + lax.ppermute(x, "sub", [(i, i ^ step) for i in range(size)])
        step *= 2
    return x


def split(x):
    hi = lax.reduce_precision(x, 8, 7)
    return hi.astype(BF), (x - hi).astype(BF)


def dot(a, b, ca, cb):
    return lax.dot_general(a, b, (((ca,), (cb,)), ((), ())), preferred_element_type=F32)


def body(queries, passages, bank, ids, counts):
    peers = lax.axis_size("dp")
    q_rows, width = queries.shape
    bank_rows = bank.shape[0]
    cap = bank_rows // 8
    places = peers * cap
    pas = passages.shape[0]
    pad = -(-(pas + 1) // 8) * 8
    blocks = q_rows // 16
    max_pos = ids.shape[1]

    first = ids[:, 0]
    rest = jnp.max(ids.reshape(blocks, 16, max_pos), 1)
    rest = jnp.where(jnp.arange(max_pos)[None, :] > 0, rest, -1).reshape(-1)
    sid = jnp.concatenate([first, rest])
    slots = sid.shape[0]
    valid = sid >= 0
    owner = jnp.where(valid, sid // bank_rows, -1)
    at = jnp.arange(slots)
    rank = jnp.sum(
        ((owner[:, None] == owner[None, :]) & (at[:, None] < at[None, :])).astype(F32), 0
    ).astype(jnp.int32)
    place = jnp.where(valid, owner * cap + rank, places)
    perm = jnp.arange(places)[:, None] == place[None, :]
    send_ids = jnp.max(jnp.where(perm, (sid % bank_rows)[None, :], -1), 1)
    q_at = jnp.arange(q_rows)
    owns = jnp.concatenate(
        [
            q_at[:, None] == q_at[None, :],
            (jnp.arange(blocks * max_pos)[:, None] // max_pos == q_at[None, :] // 16)
            & (counts[None, :] > 1),
        ]
    )
    asks = dot(perm.astype(BF), owns.astype(BF), 1, 0)
    asked = asks > 0.5

    head = jnp.broadcast_to(passages[None], (peers, pas, width))
    id_row = jnp.pad(
        send_ids.reshape(peers, 1, cap).astype(BF), ((0, 0), (0, pad - pas - 1), (0, width - cap))
    )
    heads = exchange(jnp.concatenate([head, id_row], 1))
    all_pas = heads.reshape(peers * pad, width)
    wanted = heads[:, pas, :cap].astype(F32).reshape(-1)
    pick = (wanted[:, None] == jnp.arange(bank_rows).astype(F32)[None, :]).astype(BF)
    picked = dot(pick, bank, 1, 0).astype(BF)
    fetched = exchange(picked.reshape(peers, cap, width)).reshape(places, width)
    q_send = dot(asks.astype(BF), queries, 1, 0).astype(BF)
    q_send, fetched = lax.optimization_barrier((q_send, fetched))
    q_got = exchange(q_send.reshape(peers, cap, width)).reshape(places, width)

    part = dot(all_pas, queries, 1, 1)
    pos_part = jnp.sum(jnp.where(asked, dot(fetched, queries, 1, 1), 0.0), 1)
    sums = sub_sum(jnp.concatenate([part, pos_part.reshape(-1, q_rows)])) * 50.0
    real = (jnp.arange(peers * pad) % pad < pas)[:, None]
    scores = jnp.where(real, sums[: peers * pad], -jnp.inf)
    pos = sums[peers * pad :].reshape(places, 1)
    pos_or = jnp.where(asked, pos, -jnp.inf)
    row_max = jnp.maximum(jnp.max(scores, 0), jnp.max(pos_or, 0))
    total = jnp.sum(jnp.exp(scores - row_max), 0) + jnp.sum(jnp.exp(pos_or - row_max), 0)
    log_total = row_max + jnp.log(total)
    inv_count = 1.0 / counts.astype(F32)
    losses = log_total - jnp.sum(jnp.where(asked, pos, 0.0), 0) * inv_count
    weights = jnp.exp(scores - log_total).astype(BF)
    coeffs = jnp.where(asked, jnp.exp(pos_or - log_total) - inv_count, 0.0)
    coeff = jnp.sum(coeffs, 1).reshape(peers, 1, cap)

    pas_part = dot(weights, queries, 1, 0).reshape(peers, pad, width)
    sent = jnp.where(
        jnp.arange(pad)[None, :, None] == pas,
        jnp.pad(coeff, ((0, 0), (0, 0), (0, width - cap))),
        pas_part,
    )
    sent, q_got = lax.optimization_barrier((sent, q_got))
    got = exchange(sent)

    hi, lo = split(coeffs)
    query_grad = 50.0 * (dot(weights, all_pas, 0, 0) + dot(hi, fetched, 0, 0) + dot(lo, fetched, 0, 0))
    passage_grad = 50.0 * jnp.sum(got[:, :pas], 0)
    back = got[:, pas, :cap].reshape(1, -1)
    member = jnp.where(
        wanted[None, :] == jnp.arange(bank_rows).astype(F32)[:, None], back, 0.0
    )
    hi, lo = split(member)
    bank_grad = 50.0 * (dot(hi, q_got, 1, 0) + dot(lo, q_got, 1, 0))
    return (losses, query_grad, passage_grad, bank_grad)


def solution(mesh):
    placed = (P("dp", "sub"), P("dp", "sub"), P("dp", "sub"), P("dp", None), P("dp"))
    return jax.shard_map(
        body,
        mesh=mesh,
        in_specs=placed,
        out_specs=(P("dp"), P("dp", "sub"), P("dp", "sub"), P("dp", "sub")),
        check_vma=False,
    )
```

```python
import jax
import jax.numpy as jnp
from jax import lax
from jax.sharding import PartitionSpec as P

BF = jnp.bfloat16
F32 = jnp.float32


def exchange(x):
    return lax.all_to_all(x, "dp", split_axis=0, concat_axis=0, tiled=True)


def sub_sum(x):
    size = lax.axis_size("sub")
    step = 1
    while step < size:
        x = x + lax.ppermute(x, "sub", [(i, i ^ step) for i in range(size)])
        step *= 2
    return x


def split(x):
    hi = lax.reduce_precision(x, 8, 7)
    return hi.astype(BF), (x - hi).astype(BF)


def dot(a, b, ca, cb):
    return lax.dot_general(a, b, (((ca,), (cb,)), ((), ())), preferred_element_type=F32)


def scatter_sum(x):
    size = lax.axis_size("dp")
    if size > 8 or size % 2:
        return jnp.sum(exchange(x), 0)
    me = lax.axis_index("dp")
    odd = me % 2 == 1
    even_half, odd_half = x[0::2], x[1::2]
    other = lax.ppermute(
        jnp.where(odd, even_half, odd_half), "dp", [(i, i ^ 1) for i in range(size)]
    )
    half = jnp.where(odd, odd_half, even_half) + other
    total = lax.dynamic_index_in_dim(half, me // 2, 0, False)
    parts = []
    for k in range(1, size // 2):
        part = lax.dynamic_index_in_dim(half, (me // 2) ^ k, 0, False)
        parts.append(lax.ppermute(part, "dp", [(i, i ^ (2 * k)) for i in range(size)]))
    for part in parts:
        total = total + part
    return total


def body(queries, passages, bank, ids, counts):
    peers = lax.axis_size("dp")
    q_rows, width = queries.shape
    bank_rows = bank.shape[0]
    cap = bank_rows // 8
    places = peers * cap
    pas = passages.shape[0]
    pad = -(-(pas + 1) // 8) * 8
    blocks = q_rows // 16
    max_pos = ids.shape[1]

    first = ids[:, 0]
    rest = jnp.max(ids.reshape(blocks, 16, max_pos), 1)
    rest = jnp.where(jnp.arange(max_pos)[None, :] > 0, rest, -1).reshape(-1)
    sid = jnp.concatenate([first, rest])
    slots = sid.shape[0]
    valid = sid >= 0
    owner = jnp.where(valid, sid // bank_rows, -1)
    at = jnp.arange(slots)
    rank = jnp.sum(
        ((owner[:, None] == owner[None, :]) & (at[:, None] < at[None, :])).astype(F32), 0
    ).astype(jnp.int32)
    place = jnp.where(valid, owner * cap + rank, places)
    perm = jnp.arange(places)[:, None] == place[None, :]
    send_ids = jnp.max(jnp.where(perm, (sid % bank_rows)[None, :], -1), 1)
    q_at = jnp.arange(q_rows)
    owns = jnp.concatenate(
        [
            q_at[:, None] == q_at[None, :],
            (jnp.arange(blocks * max_pos)[:, None] // max_pos == q_at[None, :] // 16)
            & (counts[None, :] > 1),
        ]
    )
    asks = dot(perm.astype(BF), owns.astype(BF), 1, 0)
    asked = asks > 0.5

    head = jnp.broadcast_to(passages[None], (peers, pas, width))
    id_row = jnp.pad(
        send_ids.reshape(peers, 1, cap).astype(BF), ((0, 0), (0, pad - pas - 1), (0, width - cap))
    )
    heads = exchange(jnp.concatenate([head, id_row], 1))
    all_pas = heads.reshape(peers * pad, width)
    wanted = heads[:, pas, :cap].astype(F32).reshape(-1)
    pick = (wanted[:, None] == jnp.arange(bank_rows).astype(F32)[None, :]).astype(BF)
    picked = dot(pick, bank, 1, 0).astype(BF)
    fetched = exchange(picked.reshape(peers, cap, width)).reshape(places, width)
    q_send = dot(asks.astype(BF), queries, 1, 0).astype(BF)
    q_send, fetched = lax.optimization_barrier((q_send, fetched))
    q_got = exchange(q_send.reshape(peers, cap, width)).reshape(places, width)

    part = dot(all_pas, queries, 1, 1)
    pos_part = jnp.sum(jnp.where(asked, dot(fetched, queries, 1, 1), 0.0), 1)
    sums = sub_sum(jnp.concatenate([part, pos_part.reshape(-1, q_rows)])) * 50.0
    real = (jnp.arange(peers * pad) % pad < pas)[:, None]
    scores = jnp.where(real, sums[: peers * pad], -jnp.inf)
    pos = sums[peers * pad :].reshape(places, 1)
    pos_or = jnp.where(asked, pos, -jnp.inf)
    row_max = jnp.maximum(jnp.max(scores, 0), jnp.max(pos_or, 0))
    total = jnp.sum(jnp.exp(scores - row_max), 0) + jnp.sum(jnp.exp(pos_or - row_max), 0)
    log_total = row_max + jnp.log(total)
    inv_count = 1.0 / counts.astype(F32)
    losses = log_total - jnp.sum(jnp.where(asked, pos, 0.0), 0) * inv_count
    weights = jnp.exp(scores - log_total).astype(BF)
    coeffs = jnp.where(asked, jnp.exp(pos_or - log_total) - inv_count, 0.0)
    coeff = jnp.sum(coeffs, 1).reshape(peers, 1, cap)
    mine = (jnp.arange(peers) == lax.axis_index("dp"))[None, :, None]
    coeff = jnp.where(mine, coeff, 0.0).reshape(peers, 1, places)

    pas_part = dot(weights, queries, 1, 0).reshape(peers, pad, width)
    sent = jnp.where(
        jnp.arange(pad)[None, :, None] == pas,
        jnp.pad(coeff, ((0, 0), (0, 0), (0, width - places))),
        pas_part,
    )
    got = scatter_sum(sent)

    hi, lo = split(coeffs)
    query_grad = 50.0 * (dot(weights, all_pas, 0, 0) + dot(hi, fetched, 0, 0) + dot(lo, fetched, 0, 0))
    passage_grad = 50.0 * got[:pas]
    back = got[pas : pas + 1, :places]
    member = jnp.where(
        wanted[None, :] == jnp.arange(bank_rows).astype(F32)[:, None], back, 0.0
    )
    hi, lo = split(member)
    bank_grad = 50.0 * (dot(hi, q_got, 1, 0) + dot(lo, q_got, 1, 0))
    return (losses, query_grad, passage_grad, bank_grad)


def solution(mesh):
    placed = (P("dp", "sub"), P("dp", "sub"), P("dp", "sub"), P("dp", None), P("dp"))
    return jax.shard_map(
        body,
        mesh=mesh,
        in_specs=placed,
        out_specs=(P("dp"), P("dp", "sub"), P("dp", "sub"), P("dp", "sub")),
        check_vma=False,
    )
```

```python
import jax
import jax.numpy as jnp
from jax import lax
from jax.sharding import PartitionSpec as P


BF = jnp.bfloat16
F32 = jnp.float32


def exchange(x, groups=None):
    return lax.all_to_all(
        x, "dp", split_axis=0, concat_axis=0, tiled=True, axis_index_groups=groups
    )


def split(x):
    hi = lax.reduce_precision(x, 8, 7)
    return hi.astype(BF), (x - hi).astype(BF)


def dot(a, b, ca, cb):
    return lax.dot_general(a, b, (((ca,), (cb,)), ((), ())), preferred_element_type=F32)


def to_pair(x):
    return lax.ppermute(x, "dp", [(i, i ^ 1) for i in range(lax.axis_size("dp"))])


def sub_sums(x):
    size, peers = lax.axis_size("sub"), lax.axis_size("dp")
    step = 1
    while 2 * step < size:
        x = x + lax.ppermute(x, "sub", [(i, i ^ step) for i in range(size)])
        step *= 2
    mine = x + lax.ppermute(x, "sub", [(i, i ^ step) for i in range(size)])
    cross = [
        (d * size + s, (d ^ 1) * size + (s ^ step)) for d in range(peers) for s in range(size)
    ]
    pair = to_pair(x)
    pair = pair + lax.ppermute(x, ("dp", "sub"), cross)
    return mine, pair


def line_groups():
    peers = lax.axis_size("dp")
    return [list(range(odd, peers, 2)) for odd in range(2)]


def scatter_sum(x):
    size = lax.axis_size("dp")
    lines = size // 2
    if lines > 4 or lines & (lines - 1):
        return jnp.sum(exchange(x, line_groups()), 0)
    line = lax.axis_index("dp") // 2
    total = lax.dynamic_index_in_dim(x, line, 0, False)
    parts = []
    for k in range(1, lines):
        part = lax.dynamic_index_in_dim(x, line ^ k, 0, False)
        parts.append(lax.ppermute(part, "dp", [(i, i ^ (2 * k)) for i in range(size)]))
    for part in parts:
        total = total + part
    return total


def owns_of(counts, max_pos):
    q_rows = counts.shape[0]
    q_at = jnp.arange(q_rows)
    return jnp.concatenate(
        [
            q_at[:, None] == q_at[None, :],
            (jnp.arange(q_rows // 16 * max_pos)[:, None] // max_pos == q_at[None, :] // 16)
            & (counts[None, :] > 1),
        ]
    )


def body(queries, passages, bank, ids, counts):
    peers = lax.axis_size("dp")
    lines = peers // 2
    me = lax.axis_index("dp")
    odd = me % 2 == 1
    q_rows, width = queries.shape
    bank_rows = bank.shape[0]
    cap = bank_rows // 8
    places = peers * cap
    pas = passages.shape[0]
    pad = -(-(pas + 1) // 8) * 8
    blocks = q_rows // 16
    max_pos = ids.shape[1]
    near = lambda x: jnp.where(odd, x[:, 1], x[:, 0])

    first = ids[:, 0]
    rest = jnp.max(ids.reshape(blocks, 16, max_pos), 1)
    rest = jnp.where(jnp.arange(max_pos)[None, :] > 0, rest, -1).reshape(-1)
    sid = jnp.concatenate([first, rest])
    slots = sid.shape[0]
    valid = sid >= 0
    owner = jnp.where(valid, sid // bank_rows, -1)
    at = jnp.arange(slots)
    rank = jnp.sum(
        ((owner[:, None] == owner[None, :]) & (at[:, None] < at[None, :])).astype(F32), 0
    ).astype(jnp.int32)
    place = jnp.where(valid, owner * cap + rank, places)
    perm = jnp.arange(places)[:, None] == place[None, :]
    send_ids = jnp.max(jnp.where(perm, (sid % bank_rows)[None, :], -1), 1)

    head = jnp.broadcast_to(passages[None], (peers, pas, width))
    id_row = jnp.pad(
        send_ids.reshape(peers, 1, cap).astype(BF), ((0, 0), (0, pad - pas - 1), (0, width - cap))
    )
    heads = exchange(jnp.concatenate([head, id_row], 1))

    notes = jnp.concatenate([place.astype(BF), counts.astype(BF)])
    notes = jnp.pad(notes[None], ((0, 7), (0, width - notes.shape[0])))
    pair_in = to_pair(jnp.concatenate([queries, notes]))
    pair_q = pair_in[:q_rows]
    pair_place = pair_in[q_rows, :slots].astype(jnp.int32)
    pair_counts = pair_in[q_rows, slots : slots + q_rows].astype(jnp.int32)
    pair_perm = jnp.arange(places)[:, None] == pair_place[None, :]
    asks = dot(perm.astype(BF), owns_of(counts, max_pos).astype(BF), 1, 0)
    pair_asks = dot(pair_perm.astype(BF), owns_of(pair_counts, max_pos).astype(BF), 1, 0)
    asks = jnp.stack([asks, pair_asks])
    asked = asks > 0.5
    both_counts = jnp.stack([counts, pair_counts]).astype(F32)[:, None, :]

    all_pas = heads.reshape(peers * pad, width)
    wanted = heads[:, pas, :cap].astype(F32).reshape(-1)
    pick = (wanted[:, None] == jnp.arange(bank_rows).astype(F32)[None, :]).astype(BF)
    picked = dot(pick, bank, 1, 0).astype(BF)
    fetched = exchange(picked.reshape(peers, cap, width)).reshape(places, width)

    send = []
    for k, rows in enumerate((queries, pair_q)):
        ask = near(asks[k].astype(BF).reshape(lines, 2, cap, q_rows)).reshape(-1, q_rows)
        send.append(dot(ask, rows, 1, 0).astype(BF).reshape(lines, 1, cap, width))
    even_send = jnp.where(odd, send[1], send[0])
    odd_send = jnp.where(odd, send[0], send[1])
    q_send = jnp.concatenate([even_send, odd_send], 1).reshape(lines, 2 * cap, width)
    q_send, fetched = lax.optimization_barrier((q_send, fetched))
    q_got = exchange(q_send, line_groups())
    q_got = q_got.reshape(places, width)

    part = dot(all_pas, queries, 1, 1)
    pos_part = jnp.sum(jnp.where(asked[0], dot(fetched, queries, 1, 1), 0.0), 1)
    mine, pair = sub_sums(jnp.concatenate([part, pos_part.reshape(-1, q_rows)]))
    sums = jnp.stack([mine, pair]) * 50.0
    real = (jnp.arange(peers * pad) % pad < pas)[None, :, None]
    scores = jnp.where(real, sums[:, : peers * pad], -jnp.inf)
    pos = sums[:, peers * pad :].reshape(2, places, 1)
    pos_or = jnp.where(asked, pos, -jnp.inf)
    row_max = jnp.maximum(jnp.max(scores, 1, keepdims=True), jnp.max(pos_or, 1, keepdims=True))
    total = jnp.sum(jnp.exp(scores - row_max), 1, keepdims=True)
    total = total + jnp.sum(jnp.exp(pos_or - row_max), 1, keepdims=True)
    log_total = row_max + jnp.log(total)
    inv_count = 1.0 / both_counts
    losses = log_total[0, 0] - jnp.sum(jnp.where(asked[0], pos[0], 0.0), 0) * inv_count[0, 0]
    weights = jnp.exp(scores - log_total).astype(BF)
    coeffs = jnp.where(asked, jnp.exp(pos_or - log_total) - inv_count, 0.0)

    pas_part = jnp.zeros((lines * pad, width), F32)
    rows = jnp.zeros((lines, peers, cap), F32)
    for k, q in enumerate((queries, pair_q)):
        near_w = near(weights[k].reshape(lines, 2, pad, q_rows)).reshape(lines * pad, q_rows)
        pas_part = pas_part + dot(near_w, q, 1, 0)
        coeff = near(jnp.sum(coeffs[k], 1).reshape(lines, 2, cap))
        source = (jnp.arange(peers) == me ^ k)[None, :, None]
        rows = jnp.where(source, coeff[:, None, :], rows)
    sent = jnp.where(
        jnp.arange(pad)[None, :, None] == pas,
        jnp.pad(rows.reshape(lines, 1, places), ((0, 0), (0, 0), (0, width - places))),
        pas_part.reshape(lines, pad, width),
    )
    got = scatter_sum(sent)

    hi, lo = split(coeffs[0])
    query_grad = 50.0 * (
        dot(weights[0], all_pas, 0, 0) + dot(hi, fetched, 0, 0) + dot(lo, fetched, 0, 0)
    )
    passage_grad = 50.0 * got[:pas]
    back = got[pas : pas + 1, :places]
    member = jnp.where(
        wanted[None, :] == jnp.arange(bank_rows).astype(F32)[:, None], back, 0.0
    )
    hi, lo = split(member)
    bank_grad = 50.0 * (dot(hi, q_got, 1, 0) + dot(lo, q_got, 1, 0))
    return (losses, query_grad, passage_grad, bank_grad)


def solution(mesh):
    placed = (P("dp", "sub"), P("dp", "sub"), P("dp", "sub"), P("dp", None), P("dp"))
    return jax.shard_map(
        body,
        mesh=mesh,
        in_specs=placed,
        out_specs=(P("dp"), P("dp", "sub"), P("dp", "sub"), P("dp", "sub")),
        check_vma=False,
    )
```

```python
import jax
import jax.numpy as jnp
from jax import lax
from jax.experimental import pallas as pl
from jax.experimental.pallas import tpu as pltpu
from jax.sharding import PartitionSpec as P


BF = jnp.bfloat16
F32 = jnp.float32


def exchange(x, groups=None):
    return lax.all_to_all(
        x, "dp", split_axis=0, concat_axis=0, tiled=True, axis_index_groups=groups
    )


def dot(a, b, ca, cb):
    return lax.dot_general(a, b, (((ca,), (cb,)), ((), ())), preferred_element_type=F32)


def to_pair(x):
    return lax.ppermute(x, "dp", [(i, i ^ 1) for i in range(lax.axis_size("dp"))])


def sub_sum(x):
    size = lax.axis_size("sub")
    step = 1
    while step < size:
        x = x + lax.ppermute(x, "sub", [(i, i ^ step) for i in range(size)])
        step *= 2
    return x


def line_groups():
    peers = lax.axis_size("dp")
    return [list(range(odd, peers, 2)) for odd in range(2)]


def scatter_sum(x):
    size = lax.axis_size("dp")
    lines = size // 2
    if lines > 4 or lines & (lines - 1):
        return [jnp.sum(exchange(x, line_groups()), 0)]
    line = lax.axis_index("dp") // 2
    total = lax.dynamic_index_in_dim(x, line, 0, False)
    parts = []
    for k in range(1, lines):
        part = lax.dynamic_index_in_dim(x, line ^ k, 0, False)
        parts.append(lax.ppermute(part, "dp", [(i, i ^ (2 * k)) for i in range(size)]))
    return [total] + parts


def iota(shape, dim):
    return lax.broadcasted_iota(jnp.int32, shape, dim)


def call(kernel, outs, flops, *args, **kw):
    size = sum(a.size * a.dtype.itemsize for a in (*args, *outs))
    cost = pl.CostEstimate(flops=flops, bytes_accessed=size, transcendentals=0)
    return pl.pallas_call(kernel, out_shape=outs, cost_estimate=cost, **kw)(*args)


VMEM = pl.BlockSpec(memory_space=pltpu.VMEM)
ROOMY = pltpu.CompilerParams(vmem_limit_bytes=16 * 2**20)


def plan(ids, passages, peers, bank_rows, pad):
    max_pos, q_rows = ids.shape
    pas, width = passages.shape
    cap = bank_rows // 8
    slots, places = 2 * q_rows, peers * cap

    def kernel(ids_ref, pas_ref, block_ref, place_ref):
        ident = (ids_ref[...] + 1).astype(F32)
        high = jnp.floor(ident / 64)
        parts = jnp.concatenate([high, ident - 64 * high]).astype(BF)
        same = (iota((q_rows, q_rows), 0) // 16 == iota((q_rows, q_rows), 1) // 16).astype(BF)
        group = jnp.dot(parts, same, preferred_element_type=F32)
        group = 64 * group[:max_pos] + group[max_pos:]
        row = iota((max_pos, q_rows), 0)
        here = (row == iota((max_pos, q_rows), 1) % max_pos) & (row > 0)
        rest = jnp.sum(jnp.where(here, group, 0.0), 0, keepdims=True)
        sid = jnp.concatenate([ident[:1], rest], 1)
        owner = jnp.floor((sid - 0.5) / bank_rows)
        local = sid - owner * bank_rows
        down, along = iota((slots, slots), 0), iota((slots, slots), 1)
        owner_col = jnp.sum(jnp.where(down == along, owner, 0.0), 1, keepdims=True)
        before = (owner_col == owner) & (down < along)
        rank = jnp.sum(before.astype(F32), 0, keepdims=True)
        place = jnp.where(sid > 0, owner * cap + rank, float(places))
        place_ref[...] = place
        perm = iota((places, slots), 0).astype(F32) == place
        id_col = jnp.sum(jnp.where(perm, local, 0.0), 1, keepdims=True) - 1
        turn = iota((places, places), 0) == iota((places, places), 1)
        id_row = jnp.sum(jnp.where(turn, id_col, 0.0), 0, keepdims=True)
        top = jnp.concatenate([pas_ref[...].astype(F32), jnp.zeros((pad - pas, width), F32)])
        below = iota((pad, width), 0) == pas
        for d in range(peers):
            tail = jnp.concatenate(
                [id_row[:, d * cap : (d + 1) * cap], jnp.zeros((1, width - cap), F32)], 1
            )
            block_ref[d] = jnp.where(below, tail, top).astype(BF)

    outs = (
        jax.ShapeDtypeStruct((peers, pad, width), BF),
        jax.ShapeDtypeStruct((1, slots), F32),
    )
    block, place = call(
        kernel,
        outs,
        10**7,
        ids,
        passages,
        in_specs=[VMEM, VMEM],
        out_specs=(VMEM, VMEM),
        name="plan",
    )
    return block, place[0].astype(jnp.int32)


def soften(sums, asks, counts, rows, where, pas, base=None):
    places, q_rows = asks.shape
    width = rows.shape[1]
    heads = sums.shape[0] - places // q_rows
    pad = -(-(pas + 1) // 8) * 8
    peers = heads // pad
    lines, cap = peers // 2, places // peers

    def kernel(where_ref, sums_ref, asks_ref, counts_ref, rows_ref, *refs):
        odd, source = where_ref[0] == 1, where_ref[1]
        total = 50.0 * sums_ref[...]
        asked = asks_ref[...] > 0.5
        real = iota((heads, q_rows), 0) % pad < pas
        scores = jnp.where(real, total[:heads], -jnp.inf)
        eye = iota((q_rows, q_rows), 0) == iota((q_rows, q_rows), 1)
        pos = jnp.concatenate(
            [
                jnp.sum(jnp.where(eye, total[j : j + 1], 0.0), 1, keepdims=True)
                for j in range(heads, heads + places // q_rows)
            ]
        )
        pos_or = jnp.where(asked, pos, -jnp.inf)
        top = jnp.maximum(
            jnp.max(scores, 0, keepdims=True), jnp.max(pos_or, 0, keepdims=True)
        )
        mass = jnp.sum(jnp.exp(scores - top), 0, keepdims=True)
        mass = mass + jnp.sum(jnp.exp(pos_or - top), 0, keepdims=True)
        log_total = top + jnp.log(mass)
        inv_count = 1.0 / counts_ref[...]
        weights = jnp.exp(scores - log_total)
        coeffs = jnp.where(asked, jnp.exp(pos_or - log_total) - inv_count, 0.0)
        if base is None:
            losses_ref, weights_ref, hi_ref, lo_ref, sent_ref = refs
            own = jnp.sum(jnp.where(asked, pos, 0.0), 0, keepdims=True)
            losses_ref[...] = log_total - own * inv_count
            weights_ref[...] = weights.astype(BF)
            hi = coeffs.astype(BF)
            hi_ref[...] = hi
            lo_ref[...] = (coeffs - hi.astype(F32)).astype(BF)
        else:
            base_ref, sent_ref = refs
        split_w = weights.reshape(lines, 2, pad, q_rows)
        near_w = jnp.where(odd, split_w[:, 1], split_w[:, 0]).reshape(lines * pad, q_rows)
        part = jnp.dot(near_w.astype(BF), rows_ref[...], preferred_element_type=F32)
        part = part.reshape(lines, pad, width)
        coeff = jnp.sum(coeffs, 1, keepdims=True)
        down, lane = iota((places, places), 0), iota((places, places), 1)
        left = jnp.where(down % cap == lane - source * cap, coeff, 0.0)
        line, at = iota((lines, places), 0), iota((lines, places), 1) // cap
        pick = (at == 2 * line + where_ref[0]).astype(BF)
        row = jnp.zeros((lines, places), F32)
        for _ in range(3):
            piece = left.astype(BF)
            left = left - piece.astype(F32)
            row = row + jnp.dot(pick, piece, preferred_element_type=F32)
        if base is not None:
            part = part + base_ref[...]
            row = row + base_ref[:, pas, :places]
        sent_ref[...] = part
        for i in range(lines):
            sent_ref[i, pas : pas + 1, :places] = row[i : i + 1]

    outs = (jax.ShapeDtypeStruct((lines, pad, width), F32),)
    args = (where, sums, asks, counts, rows)
    if base is None:
        outs = (
            jax.ShapeDtypeStruct((1, q_rows), F32),
            jax.ShapeDtypeStruct((heads, q_rows), BF),
            jax.ShapeDtypeStruct((places, q_rows), BF),
            jax.ShapeDtypeStruct((places, q_rows), BF),
        ) + outs
    else:
        args += (base,)
    return call(
        kernel,
        outs,
        10**7,
        *args,
        in_specs=[pl.BlockSpec(memory_space=pltpu.SMEM)] + [VMEM] * (len(args) - 1),
        out_specs=(VMEM,) * len(outs),
        compiler_params=ROOMY,
        name="soften" if base is None else "soften_pair",
    )


def close(parts, wanted, q_got, pas, bank_rows):
    places, width = q_got.shape
    steps = 4
    cols = width // steps
    n = len(parts)

    def kernel(*refs):
        wanted_ref, q_ref, pas_out, bank_out, pas_vmem, bank_vmem, sems = refs[n:]
        total = sum(r[...] for r in refs[:n])
        pas_vmem[...] = 50.0 * total[:pas]
        copies = [pltpu.make_async_copy(pas_vmem, pas_out, sems.at[steps])]
        copies[0].start()
        back = 50.0 * total[pas : pas + 1, :places]
        row = iota((bank_rows, places), 0).astype(F32)
        member = jnp.where(row == wanted_ref[...], back, 0.0)
        hi = member.astype(BF)
        lo = (member - hi.astype(F32)).astype(BF)
        for i in range(steps):
            at = pl.ds(i * cols, cols)
            q = q_ref[:, at]
            bank_vmem[:, at] = jnp.dot(hi, q, preferred_element_type=F32) + jnp.dot(
                lo, q, preferred_element_type=F32
            )
            copies.append(
                pltpu.make_async_copy(bank_vmem.at[:, at], bank_out.at[:, at], sems.at[i])
            )
            copies[-1].start()
        for copy in copies:
            copy.wait()

    away = pl.BlockSpec(memory_space=pl.ANY)
    return call(
        kernel,
        (
            jax.ShapeDtypeStruct((pas, width), F32),
            jax.ShapeDtypeStruct((bank_rows, width), F32),
        ),
        4 * bank_rows * places * width,
        *parts,
        wanted[None, :],
        q_got,
        in_specs=[VMEM] * (n + 2),
        out_specs=(away, away),
        scratch_shapes=[
            pltpu.VMEM((pas, width), F32),
            pltpu.VMEM((bank_rows, width), F32),
            pltpu.SemaphoreType.DMA((steps + 1,)),
        ],
        compiler_params=ROOMY,
        name="close",
    )


def owns_of(counts, max_pos):
    q_rows = counts.shape[0]
    q_at = jnp.arange(q_rows)
    return jnp.concatenate(
        [
            q_at[:, None] == q_at[None, :],
            (jnp.arange(q_rows // 16 * max_pos)[:, None] // max_pos == q_at[None, :] // 16)
            & (counts[None, :] > 1),
        ]
    )


def body(queries, passages, bank, ids, counts):
    peers = lax.axis_size("dp")
    lines = peers // 2
    me = lax.axis_index("dp")
    odd = me % 2 == 1
    q_rows, width = queries.shape
    bank_rows = bank.shape[0]
    cap = bank_rows // 8
    places = peers * cap
    pas = passages.shape[0]
    pad = -(-(pas + 1) // 8) * 8
    max_pos = ids.shape[1]
    near = lambda x: jnp.where(odd, x[:, 1], x[:, 0])

    block, place = plan(ids.T, passages, peers, bank_rows, pad)
    slots = place.shape[0]
    perm = jnp.arange(places)[:, None] == place[None, :]
    heads = exchange(block)

    notes = jnp.concatenate([place.astype(BF), counts.astype(BF)])
    notes = jnp.pad(notes[None], ((0, 7), (0, width - notes.shape[0])))
    pair_in = to_pair(jnp.concatenate([queries, notes]))
    pair_q = pair_in[:q_rows]
    pair_place = pair_in[q_rows, :slots].astype(jnp.int32)
    pair_counts = pair_in[q_rows, slots : slots + q_rows].astype(jnp.int32)
    pair_perm = jnp.arange(places)[:, None] == pair_place[None, :]
    asks = dot(perm.astype(BF), owns_of(counts, max_pos).astype(BF), 1, 0)
    pair_asks = dot(pair_perm.astype(BF), owns_of(pair_counts, max_pos).astype(BF), 1, 0)
    asks, pair_asks = asks.astype(BF), pair_asks.astype(BF)

    all_pas = heads.reshape(peers * pad, width)
    wanted = heads[:, pas, :cap].astype(F32).reshape(-1)
    pick = (wanted[:, None] == jnp.arange(bank_rows).astype(F32)[None, :]).astype(BF)
    picked = dot(pick, bank, 1, 0).astype(BF)
    fetched = exchange(picked.reshape(peers, cap, width)).reshape(places, width)

    send = []
    for ask, rows in ((asks, queries), (pair_asks, pair_q)):
        ask = near(ask.reshape(lines, 2, cap, q_rows)).reshape(-1, q_rows)
        send.append(dot(ask, rows, 1, 0).astype(BF).reshape(lines, 1, cap, width))
    even_send = jnp.where(odd, send[1], send[0])
    odd_send = jnp.where(odd, send[0], send[1])
    q_send = jnp.concatenate([even_send, odd_send], 1).reshape(lines, 2 * cap, width)
    q_send, fetched = lax.optimization_barrier((q_send, fetched))
    q_got = exchange(q_send, line_groups())
    q_got = q_got.reshape(places, width)

    part = dot(all_pas, queries, 1, 1)
    pos_part = jnp.sum(jnp.where(asks > 0.5, dot(fetched, queries, 1, 1), 0.0), 1)
    mine = sub_sum(jnp.concatenate([part, pos_part.reshape(-1, q_rows)]))
    pair = to_pair(mine)
    spot = lambda source: jnp.stack([me % 2, source]).astype(jnp.int32)
    losses, weights, hi, lo, sent = soften(
        mine, asks, counts.astype(F32)[None], queries, spot(me), pas
    )
    (sent,) = soften(
        pair, pair_asks, pair_counts.astype(F32)[None], pair_q, spot(me ^ 1), pas, sent
    )
    got = scatter_sum(sent)

    query_grad = 50.0 * (
        dot(weights, all_pas, 0, 0) + dot(hi, fetched, 0, 0) + dot(lo, fetched, 0, 0)
    )
    passage_grad, bank_grad = close(got, wanted, q_got, pas, bank_rows)
    return (losses[0], query_grad, passage_grad, bank_grad)


def solution(mesh):
    placed = (P("dp", "sub"), P("dp", "sub"), P("dp", "sub"), P("dp", None), P("dp"))
    return jax.shard_map(
        body,
        mesh=mesh,
        in_specs=placed,
        out_specs=(P("dp"), P("dp", "sub"), P("dp", "sub"), P("dp", "sub")),
        check_vma=False,
    )
```

```python
import jax
import jax.numpy as jnp
from jax import lax
from jax.experimental import pallas as pl
from jax.experimental.pallas import tpu as pltpu
from jax.sharding import PartitionSpec as P


BF = jnp.bfloat16
F32 = jnp.float32


def line_order(lines):
    return [2, 1, 3, 0] if lines == 4 else list(range(lines))


def peer_order(peers):
    return [2 * line + odd for odd in range(2) for line in line_order(peers // 2)]


def exchange(x, groups):
    return lax.all_to_all(
        x, "dp", split_axis=0, concat_axis=0, tiled=True, axis_index_groups=groups
    )


def everyone():
    return [peer_order(lax.axis_size("dp"))]


def dot(a, b, ca, cb):
    return lax.dot_general(a, b, (((ca,), (cb,)), ((), ())), preferred_element_type=F32)


def to_pair(x):
    return lax.ppermute(x, "dp", [(i, i ^ 1) for i in range(lax.axis_size("dp"))])


def sub_sum(x):
    size = lax.axis_size("sub")
    step = 1
    while step < size:
        x = x + lax.ppermute(x, "sub", [(i, i ^ step) for i in range(size)])
        step *= 2
    return x


def line_groups():
    order = line_order(lax.axis_size("dp") // 2)
    return [[2 * line + odd for line in order] for odd in range(2)]


def place_of(order, value):
    return sum(jnp.where(value == d, order.index(d), 0) for d in order)


def scatter_sum(x):
    size = lax.axis_size("dp")
    lines = size // 2
    if lines > 4 or lines & (lines - 1):
        return [jnp.sum(exchange(x, line_groups()), 0)]
    line = lax.axis_index("dp") // 2
    order = line_order(lines)
    total = lax.dynamic_index_in_dim(x, place_of(order, line), 0, False)
    parts = []
    for k in range(1, lines):
        part = lax.dynamic_index_in_dim(x, place_of(order, line ^ k), 0, False)
        parts.append(lax.ppermute(part, "dp", [(i, i ^ (2 * k)) for i in range(size)]))
    return [total] + parts


def iota(shape, dim):
    return lax.broadcasted_iota(jnp.int32, shape, dim)


def call(kernel, outs, flops, *args, **kw):
    size = sum(a.size * a.dtype.itemsize for a in (*args, *outs))
    cost = pl.CostEstimate(flops=flops, bytes_accessed=size, transcendentals=0)
    return pl.pallas_call(kernel, out_shape=outs, cost_estimate=cost, **kw)(*args)


VMEM = pl.BlockSpec(memory_space=pltpu.VMEM)
ROOMY = pltpu.CompilerParams(vmem_limit_bytes=16 * 2**20)


def plan(ids, passages, peers, bank_rows, pad):
    max_pos, q_rows = ids.shape
    pas, width = passages.shape
    cap = bank_rows // 8
    slots, places = 2 * q_rows, peers * cap
    order = peer_order(peers)

    def kernel(ids_ref, pas_ref, block_ref, place_ref):
        ident = (ids_ref[...] + 1).astype(F32)
        high = jnp.floor(ident / 64)
        parts = jnp.concatenate([high, ident - 64 * high]).astype(BF)
        same = (iota((q_rows, q_rows), 0) // 16 == iota((q_rows, q_rows), 1) // 16).astype(BF)
        group = jnp.dot(parts, same, preferred_element_type=F32)
        group = 64 * group[:max_pos] + group[max_pos:]
        row = iota((max_pos, q_rows), 0)
        here = (row == iota((max_pos, q_rows), 1) % max_pos) & (row > 0)
        rest = jnp.sum(jnp.where(here, group, 0.0), 0, keepdims=True)
        sid = jnp.concatenate([ident[:1], rest], 1)
        owner = jnp.floor((sid - 0.5) / bank_rows)
        local = sid - owner * bank_rows
        down, along = iota((slots, slots), 0), iota((slots, slots), 1)
        owner_col = jnp.sum(jnp.where(down == along, owner, 0.0), 1, keepdims=True)
        before = (owner_col == owner) & (down < along)
        rank = jnp.sum(before.astype(F32), 0, keepdims=True)
        spot = jnp.zeros_like(owner)
        for j, d in enumerate(order):
            spot = jnp.where(owner == d, float(j), spot)
        place = jnp.where(sid > 0, spot * cap + rank, float(places))
        place_ref[...] = place
        perm = iota((places, slots), 0).astype(F32) == place
        id_col = jnp.sum(jnp.where(perm, local, 0.0), 1, keepdims=True) - 1
        turn = iota((places, places), 0) == iota((places, places), 1)
        id_row = jnp.sum(jnp.where(turn, id_col, 0.0), 0, keepdims=True)
        top = jnp.concatenate([pas_ref[...].astype(F32), jnp.zeros((pad - pas, width), F32)])
        below = iota((pad, width), 0) == pas
        for d in range(peers):
            tail = jnp.concatenate(
                [id_row[:, d * cap : (d + 1) * cap], jnp.zeros((1, width - cap), F32)], 1
            )
            block_ref[d] = jnp.where(below, tail, top).astype(BF)

    outs = (
        jax.ShapeDtypeStruct((peers, pad, width), BF),
        jax.ShapeDtypeStruct((1, slots), F32),
    )
    block, place = call(
        kernel,
        outs,
        10**7,
        ids,
        passages,
        in_specs=[VMEM, VMEM],
        out_specs=(VMEM, VMEM),
        name="plan",
    )
    return block, place[0].astype(jnp.int32)


def soften(sums, asks, counts, rows, where, pas, base=None):
    places, q_rows = asks.shape
    width = rows.shape[1]
    heads = sums.shape[0] - places // q_rows
    pad = -(-(pas + 1) // 8) * 8
    peers = heads // pad
    lines, cap = peers // 2, places // peers

    def kernel(where_ref, sums_ref, asks_ref, counts_ref, rows_ref, *refs):
        odd, source = where_ref[0] == 1, where_ref[1]
        total = 50.0 * sums_ref[...]
        asked = asks_ref[...] > 0.5
        real = iota((heads, q_rows), 0) % pad < pas
        scores = jnp.where(real, total[:heads], -jnp.inf)
        eye = iota((q_rows, q_rows), 0) == iota((q_rows, q_rows), 1)
        pos = jnp.concatenate(
            [
                jnp.sum(jnp.where(eye, total[j : j + 1], 0.0), 1, keepdims=True)
                for j in range(heads, heads + places // q_rows)
            ]
        )
        pos_or = jnp.where(asked, pos, -jnp.inf)
        top = jnp.maximum(
            jnp.max(scores, 0, keepdims=True), jnp.max(pos_or, 0, keepdims=True)
        )
        mass = jnp.sum(jnp.exp(scores - top), 0, keepdims=True)
        mass = mass + jnp.sum(jnp.exp(pos_or - top), 0, keepdims=True)
        log_total = top + jnp.log(mass)
        inv_count = 1.0 / counts_ref[...]
        weights = jnp.exp(scores - log_total)
        coeffs = jnp.where(asked, jnp.exp(pos_or - log_total) - inv_count, 0.0)
        if base is None:
            losses_ref, weights_ref, hi_ref, lo_ref, sent_ref = refs
            own = jnp.sum(jnp.where(asked, pos, 0.0), 0, keepdims=True)
            losses_ref[...] = log_total - own * inv_count
            weights_ref[...] = weights.astype(BF)
            hi = coeffs.astype(BF)
            hi_ref[...] = hi
            lo_ref[...] = (coeffs - hi.astype(F32)).astype(BF)
        else:
            base_ref, sent_ref = refs
        half = lines * pad
        near_w = jnp.where(odd, weights[half:], weights[:half])
        part = jnp.dot(near_w.astype(BF), rows_ref[...], preferred_element_type=F32)
        part = part.reshape(lines, pad, width)
        coeff = jnp.sum(coeffs, 1, keepdims=True)
        down, lane = iota((places, places), 0), iota((places, places), 1)
        left = jnp.where(down % cap == lane - source * cap, coeff, 0.0)
        line, at = iota((lines, places), 0), iota((lines, places), 1) // cap
        pick = (at == line + lines * where_ref[0]).astype(BF)
        row = jnp.zeros((lines, places), F32)
        for _ in range(3):
            piece = left.astype(BF)
            left = left - piece.astype(F32)
            row = row + jnp.dot(pick, piece, preferred_element_type=F32)
        if base is not None:
            part = part + base_ref[...]
            row = row + base_ref[:, pas, :places]
        sent_ref[...] = part
        for i in range(lines):
            sent_ref[i, pas : pas + 1, :places] = row[i : i + 1]

    outs = (jax.ShapeDtypeStruct((lines, pad, width), F32),)
    args = (where, sums, asks, counts, rows)
    if base is None:
        outs = (
            jax.ShapeDtypeStruct((1, q_rows), F32),
            jax.ShapeDtypeStruct((heads, q_rows), BF),
            jax.ShapeDtypeStruct((places, q_rows), BF),
            jax.ShapeDtypeStruct((places, q_rows), BF),
        ) + outs
    else:
        args += (base,)
    return call(
        kernel,
        outs,
        10**7,
        *args,
        in_specs=[pl.BlockSpec(memory_space=pltpu.SMEM)] + [VMEM] * (len(args) - 1),
        out_specs=(VMEM,) * len(outs),
        compiler_params=ROOMY,
        name="soften" if base is None else "soften_pair",
    )


def close(parts, wanted, q_got, pas, bank_rows):
    places, width = q_got.shape
    steps = 4
    cols = width // steps
    n = len(parts)

    def kernel(*refs):
        wanted_ref, q_ref, pas_out, bank_out, pas_vmem, bank_vmem, sems = refs[n:]
        total = sum(r[...] for r in refs[:n])
        pas_vmem[...] = 50.0 * total[:pas]
        copies = [pltpu.make_async_copy(pas_vmem, pas_out, sems.at[steps])]
        copies[0].start()
        back = 50.0 * total[pas : pas + 1, :places]
        row = iota((bank_rows, places), 0).astype(F32)
        member = jnp.where(row == wanted_ref[...], back, 0.0)
        hi = member.astype(BF)
        lo = (member - hi.astype(F32)).astype(BF)
        for i in range(steps):
            at = pl.ds(i * cols, cols)
            q = q_ref[:, at]
            bank_vmem[:, at] = jnp.dot(hi, q, preferred_element_type=F32) + jnp.dot(
                lo, q, preferred_element_type=F32
            )
            copies.append(
                pltpu.make_async_copy(bank_vmem.at[:, at], bank_out.at[:, at], sems.at[i])
            )
            copies[-1].start()
        for copy in copies:
            copy.wait()

    away = pl.BlockSpec(memory_space=pl.ANY)
    return call(
        kernel,
        (
            jax.ShapeDtypeStruct((pas, width), F32),
            jax.ShapeDtypeStruct((bank_rows, width), F32),
        ),
        4 * bank_rows * places * width,
        *parts,
        wanted[None, :],
        q_got,
        in_specs=[VMEM] * (n + 2),
        out_specs=(away, away),
        scratch_shapes=[
            pltpu.VMEM((pas, width), F32),
            pltpu.VMEM((bank_rows, width), F32),
            pltpu.SemaphoreType.DMA((steps + 1,)),
        ],
        compiler_params=ROOMY,
        name="close",
    )


def owns_of(counts, max_pos):
    q_rows = counts.shape[0]
    q_at = jnp.arange(q_rows)
    return jnp.concatenate(
        [
            q_at[:, None] == q_at[None, :],
            (jnp.arange(q_rows // 16 * max_pos)[:, None] // max_pos == q_at[None, :] // 16)
            & (counts[None, :] > 1),
        ]
    )


def body(queries, passages, bank, ids, counts):
    peers = lax.axis_size("dp")
    lines = peers // 2
    me = lax.axis_index("dp")
    odd = me % 2 == 1
    q_rows, width = queries.shape
    bank_rows = bank.shape[0]
    cap = bank_rows // 8
    places = peers * cap
    pas = passages.shape[0]
    pad = -(-(pas + 1) // 8) * 8
    max_pos = ids.shape[1]
    half = places // 2
    near = lambda x: jnp.where(odd, x[half:], x[:half])

    block, place = plan(ids.T, passages, peers, bank_rows, pad)
    slots = place.shape[0]
    perm = jnp.arange(places)[:, None] == place[None, :]
    heads = exchange(block, everyone())

    notes = jnp.concatenate([place.astype(BF), counts.astype(BF)])
    notes = jnp.pad(notes[None], ((0, 7), (0, width - notes.shape[0])))
    pair_in = to_pair(jnp.concatenate([queries, notes]))
    pair_q = pair_in[:q_rows]
    pair_place = pair_in[q_rows, :slots].astype(jnp.int32)
    pair_counts = pair_in[q_rows, slots : slots + q_rows].astype(jnp.int32)
    pair_perm = jnp.arange(places)[:, None] == pair_place[None, :]
    asks = dot(perm.astype(BF), owns_of(counts, max_pos).astype(BF), 1, 0)
    pair_asks = dot(pair_perm.astype(BF), owns_of(pair_counts, max_pos).astype(BF), 1, 0)
    asks, pair_asks = asks.astype(BF), pair_asks.astype(BF)

    all_pas = heads.reshape(peers * pad, width)
    wanted = heads[:, pas, :cap].astype(F32).reshape(-1)
    pick = (wanted[:, None] == jnp.arange(bank_rows).astype(F32)[None, :]).astype(BF)
    picked = dot(pick, bank, 1, 0).astype(BF)
    fetched = exchange(picked.reshape(peers, cap, width), everyone()).reshape(places, width)

    send = []
    for ask, rows in ((asks, queries), (pair_asks, pair_q)):
        send.append(dot(near(ask), rows, 1, 0).astype(BF).reshape(lines, 1, cap, width))
    even_send = jnp.where(odd, send[1], send[0])
    odd_send = jnp.where(odd, send[0], send[1])
    q_send = jnp.concatenate([even_send, odd_send], 1).reshape(lines, 2 * cap, width)
    q_send, fetched = lax.optimization_barrier((q_send, fetched))
    q_got = exchange(q_send, line_groups())
    q_got = q_got.reshape(places, width)

    part = dot(all_pas, queries, 1, 1)
    pos_part = jnp.sum(jnp.where(asks > 0.5, dot(fetched, queries, 1, 1), 0.0), 1)
    mine = sub_sum(jnp.concatenate([part, pos_part.reshape(-1, q_rows)]))
    pair = to_pair(mine)
    at = 2 * place_of(line_order(lines), me // 2)
    spot = lambda source: jnp.stack([me % 2, at + source % 2]).astype(jnp.int32)
    losses, weights, hi, lo, sent = soften(
        mine, asks, counts.astype(F32)[None], queries, spot(me), pas
    )
    (sent,) = soften(
        pair, pair_asks, pair_counts.astype(F32)[None], pair_q, spot(me ^ 1), pas, sent
    )
    got = scatter_sum(sent)

    query_grad = 50.0 * (
        dot(weights, all_pas, 0, 0) + dot(hi, fetched, 0, 0) + dot(lo, fetched, 0, 0)
    )
    wanted = wanted.reshape(2, lines, cap).swapaxes(0, 1).reshape(-1)
    passage_grad, bank_grad = close(got, wanted, q_got, pas, bank_rows)
    return (losses[0], query_grad, passage_grad, bank_grad)


def solution(mesh):
    placed = (P("dp", "sub"), P("dp", "sub"), P("dp", "sub"), P("dp", None), P("dp"))
    return jax.shard_map(
        body,
        mesh=mesh,
        in_specs=placed,
        out_specs=(P("dp"), P("dp", "sub"), P("dp", "sub"), P("dp", "sub")),
        check_vma=False,
    )
```

```python
import jax
import jax.numpy as jnp
from jax import lax
from jax.experimental import pallas as pl
from jax.experimental.pallas import tpu as pltpu
from jax.sharding import PartitionSpec as P


BF = jnp.bfloat16
F32 = jnp.float32


def line_order(lines):
    return [2, 0, 1, 3] if lines == 4 else list(range(lines))


def peer_order(peers):
    return [2 * line + odd for odd in range(2) for line in line_order(peers // 2)]


def exchange(x, groups):
    return lax.all_to_all(
        x, "dp", split_axis=0, concat_axis=0, tiled=True, axis_index_groups=groups
    )


def everyone():
    return [peer_order(lax.axis_size("dp"))]


def dot(a, b, ca, cb):
    return lax.dot_general(a, b, (((ca,), (cb,)), ((), ())), preferred_element_type=F32)


def to_pair(x):
    return lax.ppermute(x, "dp", [(i, i ^ 1) for i in range(lax.axis_size("dp"))])


def sub_sum(x):
    size = lax.axis_size("sub")
    step = 1
    while step < size:
        x = x + lax.ppermute(x, "sub", [(i, i ^ step) for i in range(size)])
        step *= 2
    return x


def line_groups():
    order = line_order(lax.axis_size("dp") // 2)
    return [[2 * line + odd for line in order] for odd in range(2)]


def place_of(order, value):
    return sum(jnp.where(value == d, order.index(d), 0) for d in order)


def scatter_sum(x):
    size = lax.axis_size("dp")
    lines = size // 2
    if lines > 4 or lines & (lines - 1):
        return [jnp.sum(exchange(x, line_groups()), 0)]
    line = lax.axis_index("dp") // 2
    order = line_order(lines)
    total = lax.dynamic_index_in_dim(x, place_of(order, line), 0, False)
    parts = []
    for k in range(lines - 1, 0, -1):
        part = lax.dynamic_index_in_dim(x, place_of(order, line ^ k), 0, False)
        parts.append(lax.ppermute(part, "dp", [(i, i ^ (2 * k)) for i in range(size)]))
    return [total] + parts


def iota(shape, dim):
    return lax.broadcasted_iota(jnp.int32, shape, dim)


def call(kernel, outs, flops, *args, **kw):
    size = sum(a.size * a.dtype.itemsize for a in (*args, *outs))
    cost = pl.CostEstimate(flops=flops, bytes_accessed=size, transcendentals=0)
    return pl.pallas_call(kernel, out_shape=outs, cost_estimate=cost, **kw)(*args)


VMEM = pl.BlockSpec(memory_space=pltpu.VMEM)
ROOMY = pltpu.CompilerParams(vmem_limit_bytes=16 * 2**20)


def plan(ids, passages, peers, bank_rows, pad):
    max_pos, q_rows = ids.shape
    pas, width = passages.shape
    cap = bank_rows // 8
    slots, places = 2 * q_rows, peers * cap
    order = peer_order(peers)

    def kernel(ids_ref, pas_ref, block_ref, place_ref):
        ident = (ids_ref[...] + 1).astype(F32)
        high = jnp.floor(ident / 64)
        parts = jnp.concatenate([high, ident - 64 * high]).astype(BF)
        same = (iota((q_rows, q_rows), 0) // 16 == iota((q_rows, q_rows), 1) // 16).astype(BF)
        group = jnp.dot(parts, same, preferred_element_type=F32)
        group = 64 * group[:max_pos] + group[max_pos:]
        row = iota((max_pos, q_rows), 0)
        here = (row == iota((max_pos, q_rows), 1) % max_pos) & (row > 0)
        rest = jnp.sum(jnp.where(here, group, 0.0), 0, keepdims=True)
        sid = jnp.concatenate([ident[:1], rest], 1)
        owner = jnp.floor((sid - 0.5) / bank_rows)
        local = sid - owner * bank_rows
        down, along = iota((slots, slots), 0), iota((slots, slots), 1)
        owner_col = jnp.sum(jnp.where(down == along, owner, 0.0), 1, keepdims=True)
        before = (owner_col == owner) & (down < along)
        rank = jnp.sum(before.astype(F32), 0, keepdims=True)
        spot = jnp.zeros_like(owner)
        for j, d in enumerate(order):
            spot = jnp.where(owner == d, float(j), spot)
        place = jnp.where(sid > 0, spot * cap + rank, float(places))
        place_ref[...] = place
        perm = iota((places, slots), 0).astype(F32) == place
        id_col = jnp.sum(jnp.where(perm, local, 0.0), 1, keepdims=True) - 1
        turn = iota((places, places), 0) == iota((places, places), 1)
        id_row = jnp.sum(jnp.where(turn, id_col, 0.0), 0, keepdims=True)
        top = jnp.concatenate([pas_ref[...].astype(F32), jnp.zeros((pad - pas, width), F32)])
        below = iota((pad, width), 0) == pas
        for d in range(peers):
            tail = jnp.concatenate(
                [id_row[:, d * cap : (d + 1) * cap], jnp.zeros((1, width - cap), F32)], 1
            )
            block_ref[d] = jnp.where(below, tail, top).astype(BF)

    outs = (
        jax.ShapeDtypeStruct((peers, pad, width), BF),
        jax.ShapeDtypeStruct((1, slots), F32),
    )
    block, place = call(
        kernel,
        outs,
        10**7,
        ids,
        passages,
        in_specs=[VMEM, VMEM],
        out_specs=(VMEM, VMEM),
        name="plan",
    )
    return block, place[0].astype(jnp.int32)


def soften(sums, asks, counts, rows, where, pas, base=None):
    places, q_rows = asks.shape
    width = rows.shape[1]
    heads = sums.shape[0] - places // q_rows
    pad = -(-(pas + 1) // 8) * 8
    peers = heads // pad
    lines, cap = peers // 2, places // peers

    def kernel(where_ref, sums_ref, asks_ref, counts_ref, rows_ref, *refs):
        odd, source = where_ref[0] == 1, where_ref[1]
        total = 50.0 * sums_ref[...]
        asked = asks_ref[...] > 0.5
        real = iota((heads, q_rows), 0) % pad < pas
        scores = jnp.where(real, total[:heads], -jnp.inf)
        eye = iota((q_rows, q_rows), 0) == iota((q_rows, q_rows), 1)
        pos = jnp.concatenate(
            [
                jnp.sum(jnp.where(eye, total[j : j + 1], 0.0), 1, keepdims=True)
                for j in range(heads, heads + places // q_rows)
            ]
        )
        pos_or = jnp.where(asked, pos, -jnp.inf)
        top = jnp.maximum(
            jnp.max(scores, 0, keepdims=True), jnp.max(pos_or, 0, keepdims=True)
        )
        score_mass, pos_mass = jnp.exp(scores - top), jnp.exp(pos_or - top)
        mass = jnp.sum(score_mass, 0, keepdims=True) + jnp.sum(pos_mass, 0, keepdims=True)
        inv_mass = 1.0 / mass
        inv_count = 1.0 / counts_ref[...]
        weights = score_mass * inv_mass
        coeffs = jnp.where(asked, pos_mass * inv_mass - inv_count, 0.0)
        if base is None:
            losses_ref, weights_ref, hi_ref, lo_ref, sent_ref = refs
            own = jnp.sum(jnp.where(asked, pos, 0.0), 0, keepdims=True)
            losses_ref[...] = top + jnp.log(mass) - own * inv_count
            weights_ref[...] = weights.astype(BF)
            hi = coeffs.astype(BF)
            hi_ref[...] = hi
            lo_ref[...] = (coeffs - hi.astype(F32)).astype(BF)
        else:
            base_ref, sent_ref = refs
        half = lines * pad
        near_w = jnp.where(odd, weights[half:], weights[:half])
        part = jnp.dot(near_w.astype(BF), rows_ref[...], preferred_element_type=F32)
        part = part.reshape(lines, pad, width)
        coeff = jnp.sum(coeffs, 1, keepdims=True)
        if cap % 8 == 0 and 128 % cap == 0 and places % 128 == 0:
            mid = places // 2
            near_c = jnp.where(odd, coeff[mid:], coeff[:mid])
            fits = iota((mid, 128), 0) % cap == iota((mid, 128), 1) % cap
            left = jnp.where(fits, near_c, 0.0).reshape(lines, cap, 128)
            row = jnp.concatenate([jnp.sum(left, 1)] * (places // 128), 1)
            row = jnp.where(iota((lines, places), 1) // cap == source, row, 0.0)
        else:
            down, lane = iota((places, places), 0), iota((places, places), 1)
            left = jnp.where(down % cap == lane - source * cap, coeff, 0.0)
            line, at = iota((lines, places), 0), iota((lines, places), 1) // cap
            pick = (at == line + lines * where_ref[0]).astype(BF)
            row = jnp.zeros((lines, places), F32)
            for _ in range(3):
                piece = left.astype(BF)
                left = left - piece.astype(F32)
                row = row + jnp.dot(pick, piece, preferred_element_type=F32)
        if base is not None:
            part = part + base_ref[...]
            row = row + base_ref[:, pas, :places]
        sent_ref[...] = part
        for i in range(lines):
            sent_ref[i, pas : pas + 1, :places] = row[i : i + 1]

    outs = (jax.ShapeDtypeStruct((lines, pad, width), F32),)
    args = (where, sums, asks, counts, rows)
    if base is None:
        outs = (
            jax.ShapeDtypeStruct((1, q_rows), F32),
            jax.ShapeDtypeStruct((heads, q_rows), BF),
            jax.ShapeDtypeStruct((places, q_rows), BF),
            jax.ShapeDtypeStruct((places, q_rows), BF),
        ) + outs
    else:
        args += (base,)
    return call(
        kernel,
        outs,
        10**7,
        *args,
        in_specs=[pl.BlockSpec(memory_space=pltpu.SMEM)] + [VMEM] * (len(args) - 1),
        out_specs=(VMEM,) * len(outs),
        compiler_params=ROOMY,
        name="soften" if base is None else "soften_pair",
    )


def close(parts, wanted, q_got, pas, bank_rows):
    places, width = q_got.shape
    steps = 4
    cols = width // steps
    n = len(parts)

    def kernel(*refs):
        wanted_ref, q_ref, pas_out, bank_out, pas_vmem, bank_vmem, sems = refs[n:]
        total = sum(r[...] for r in refs[:n])
        pas_vmem[...] = 50.0 * total[:pas]
        copies = [pltpu.make_async_copy(pas_vmem, pas_out, sems.at[steps])]
        copies[0].start()
        back = 50.0 * total[pas : pas + 1, :places]
        row = iota((bank_rows, places), 0).astype(F32)
        member = jnp.where(row == wanted_ref[...], back, 0.0)
        hi = member.astype(BF)
        lo = (member - hi.astype(F32)).astype(BF)
        for i in range(steps):
            at = pl.ds(i * cols, cols)
            q = q_ref[:, at]
            bank_vmem[:, at] = jnp.dot(hi, q, preferred_element_type=F32) + jnp.dot(
                lo, q, preferred_element_type=F32
            )
            copies.append(
                pltpu.make_async_copy(bank_vmem.at[:, at], bank_out.at[:, at], sems.at[i])
            )
            copies[-1].start()
        for copy in copies:
            copy.wait()

    away = pl.BlockSpec(memory_space=pl.ANY)
    return call(
        kernel,
        (
            jax.ShapeDtypeStruct((pas, width), F32),
            jax.ShapeDtypeStruct((bank_rows, width), F32),
        ),
        4 * bank_rows * places * width,
        *parts,
        wanted[None, :],
        q_got,
        in_specs=[VMEM] * (n + 2),
        out_specs=(away, away),
        scratch_shapes=[
            pltpu.VMEM((pas, width), F32),
            pltpu.VMEM((bank_rows, width), F32),
            pltpu.SemaphoreType.DMA((steps + 1,)),
        ],
        compiler_params=ROOMY,
        name="close",
    )


def owns_of(counts, max_pos):
    q_rows = counts.shape[0]
    q_at = jnp.arange(q_rows)
    return jnp.concatenate(
        [
            q_at[:, None] == q_at[None, :],
            (jnp.arange(q_rows // 16 * max_pos)[:, None] // max_pos == q_at[None, :] // 16)
            & (counts[None, :] > 1),
        ]
    )


def body(queries, passages, bank, ids, counts):
    peers = lax.axis_size("dp")
    lines = peers // 2
    me = lax.axis_index("dp")
    odd = me % 2 == 1
    q_rows, width = queries.shape
    bank_rows = bank.shape[0]
    cap = bank_rows // 8
    places = peers * cap
    pas = passages.shape[0]
    pad = -(-(pas + 1) // 8) * 8
    max_pos = ids.shape[1]
    half = places // 2
    near = lambda x: jnp.where(odd, x[half:], x[:half])

    block, place = plan(ids.T, passages, peers, bank_rows, pad)
    slots = place.shape[0]
    perm = jnp.arange(places)[:, None] == place[None, :]
    heads = exchange(block, everyone())

    notes = jnp.concatenate([place.astype(BF), counts.astype(BF)])
    notes = jnp.pad(notes[None], ((0, 7), (0, width - notes.shape[0])))
    pair_in = to_pair(jnp.concatenate([queries, notes]))
    pair_q = pair_in[:q_rows]
    pair_place = pair_in[q_rows, :slots].astype(jnp.int32)
    pair_counts = pair_in[q_rows, slots : slots + q_rows].astype(jnp.int32)
    pair_perm = jnp.arange(places)[:, None] == pair_place[None, :]
    asks = dot(perm.astype(BF), owns_of(counts, max_pos).astype(BF), 1, 0)
    pair_asks = dot(pair_perm.astype(BF), owns_of(pair_counts, max_pos).astype(BF), 1, 0)
    asks, pair_asks = asks.astype(BF), pair_asks.astype(BF)

    all_pas = heads.reshape(peers * pad, width)
    wanted = heads[:, pas, :cap].astype(F32).reshape(-1)
    pick = (wanted[:, None] == jnp.arange(bank_rows).astype(F32)[None, :]).astype(BF)
    picked = dot(pick, bank, 1, 0).astype(BF)
    fetched = exchange(picked.reshape(peers, cap, width), everyone()).reshape(places, width)

    send = []
    for ask, rows in ((asks, queries), (pair_asks, pair_q)):
        send.append(dot(near(ask), rows, 1, 0).astype(BF).reshape(lines, 1, cap, width))
    even_send = jnp.where(odd, send[1], send[0])
    odd_send = jnp.where(odd, send[0], send[1])
    q_send = jnp.concatenate([even_send, odd_send], 1).reshape(lines, 2 * cap, width)
    q_send, fetched = lax.optimization_barrier((q_send, fetched))
    q_got = exchange(q_send, line_groups())
    q_got = q_got.reshape(places, width)

    part = dot(all_pas, queries, 1, 1)
    pos_part = jnp.sum(jnp.where(asks > 0.5, dot(fetched, queries, 1, 1), 0.0), 1)
    mine = sub_sum(jnp.concatenate([part, pos_part.reshape(-1, q_rows)]))
    pair = to_pair(mine)
    at = 2 * place_of(line_order(lines), me // 2)
    spot = lambda source: jnp.stack([me % 2, at + source % 2]).astype(jnp.int32)
    losses, weights, hi, lo, sent = soften(
        mine, asks, counts.astype(F32)[None], queries, spot(me), pas
    )
    (sent,) = soften(
        pair, pair_asks, pair_counts.astype(F32)[None], pair_q, spot(me ^ 1), pas, sent
    )
    got = scatter_sum(sent)

    query_grad = 50.0 * (
        dot(weights, all_pas, 0, 0) + dot(hi, fetched, 0, 0) + dot(lo, fetched, 0, 0)
    )
    wanted = wanted.reshape(2, lines, cap).swapaxes(0, 1).reshape(-1)
    passage_grad, bank_grad = close(got, wanted, q_got, pas, bank_rows)
    return (losses[0], query_grad, passage_grad, bank_grad)


def solution(mesh):
    placed = (P("dp", "sub"), P("dp", "sub"), P("dp", "sub"), P("dp", None), P("dp"))
    return jax.shard_map(
        body,
        mesh=mesh,
        in_specs=placed,
        out_specs=(P("dp"), P("dp", "sub"), P("dp", "sub"), P("dp", "sub")),
        check_vma=False,
    )
```

```python
import jax
import jax.numpy as jnp
from jax import lax
from jax.experimental import pallas as pl
from jax.experimental.pallas import tpu as pltpu
from jax.sharding import PartitionSpec as P


BF = jnp.bfloat16
F32 = jnp.float32


def line_order(lines):
    return [2, 0, 1, 3] if lines == 4 else list(range(lines))


def peer_order(peers):
    return [2 * line + odd for odd in range(2) for line in line_order(peers // 2)]


def exchange(x, groups):
    return lax.all_to_all(
        x, "dp", split_axis=0, concat_axis=0, tiled=True, axis_index_groups=groups
    )


def everyone():
    return [peer_order(lax.axis_size("dp"))]


def dot(a, b, ca, cb):
    return lax.dot_general(a, b, (((ca,), (cb,)), ((), ())), preferred_element_type=F32)


def to_pair(x):
    return lax.ppermute(x, "dp", [(i, i ^ 1) for i in range(lax.axis_size("dp"))])


def sub_sum(x):
    size = lax.axis_size("sub")
    step = 1
    while step < size:
        x = x + lax.ppermute(x, "sub", [(i, i ^ step) for i in range(size)])
        step *= 2
    return x


def line_groups():
    order = line_order(lax.axis_size("dp") // 2)
    return [[2 * line + odd for line in order] for odd in range(2)]


def place_of(order, value):
    return sum(jnp.where(value == d, order.index(d), 0) for d in order)


def scatter_sum(x):
    size = lax.axis_size("dp")
    lines = size // 2
    if lines > 4 or lines & (lines - 1):
        return [jnp.sum(exchange(x, line_groups()), 0)]
    line = lax.axis_index("dp") // 2
    order = line_order(lines)
    total = lax.dynamic_index_in_dim(x, place_of(order, line), 0, False)
    parts = []
    for k in ([3, 1, 2] if lines == 4 else range(1, lines)):
        part = lax.dynamic_index_in_dim(x, place_of(order, line ^ k), 0, False)
        parts.append(lax.ppermute(part, "dp", [(i, i ^ (2 * k)) for i in range(size)]))
    return [total] + parts


def iota(shape, dim):
    return lax.broadcasted_iota(jnp.int32, shape, dim)


def call(kernel, outs, flops, *args, **kw):
    size = sum(a.size * a.dtype.itemsize for a in (*args, *outs))
    cost = pl.CostEstimate(flops=flops, bytes_accessed=size, transcendentals=0)
    return pl.pallas_call(kernel, out_shape=outs, cost_estimate=cost, **kw)(*args)


VMEM = pl.BlockSpec(memory_space=pltpu.VMEM)
ROOMY = pltpu.CompilerParams(vmem_limit_bytes=16 * 2**20)


def plan(ids, passages, peers, bank_rows, pad):
    max_pos, q_rows = ids.shape
    pas, width = passages.shape
    cap = bank_rows // 8
    slots, places = 2 * q_rows, peers * cap
    order = peer_order(peers)

    def kernel(ids_ref, pas_ref, block_ref, place_ref):
        ident = (ids_ref[...] + 1).astype(F32)
        high = jnp.floor(ident / 64)
        parts = jnp.concatenate([high, ident - 64 * high]).astype(BF)
        same = (iota((q_rows, q_rows), 0) // 16 == iota((q_rows, q_rows), 1) // 16).astype(BF)
        group = jnp.dot(parts, same, preferred_element_type=F32)
        group = 64 * group[:max_pos] + group[max_pos:]
        row = iota((max_pos, q_rows), 0)
        here = (row == iota((max_pos, q_rows), 1) % max_pos) & (row > 0)
        rest = jnp.sum(jnp.where(here, group, 0.0), 0, keepdims=True)
        sid = jnp.concatenate([ident[:1], rest], 1)
        owner = jnp.floor((sid - 0.5) / bank_rows)
        local = sid - owner * bank_rows
        down, along = iota((slots, slots), 0), iota((slots, slots), 1)
        owner_col = jnp.sum(jnp.where(down == along, owner, 0.0), 1, keepdims=True)
        before = (owner_col == owner) & (down < along)
        rank = jnp.sum(before.astype(F32), 0, keepdims=True)
        spot = jnp.zeros_like(owner)
        for j, d in enumerate(order):
            spot = jnp.where(owner == d, float(j), spot)
        place = jnp.where(sid > 0, spot * cap + rank, float(places))
        place_ref[...] = place
        perm = iota((places, slots), 0).astype(F32) == place
        id_col = jnp.sum(jnp.where(perm, local, 0.0), 1, keepdims=True) - 1
        turn = iota((places, places), 0) == iota((places, places), 1)
        id_row = jnp.sum(jnp.where(turn, id_col, 0.0), 0, keepdims=True)
        top = jnp.concatenate([pas_ref[...].astype(F32), jnp.zeros((pad - pas, width), F32)])
        below = iota((pad, width), 0) == pas
        for d in range(peers):
            tail = jnp.concatenate(
                [id_row[:, d * cap : (d + 1) * cap], jnp.zeros((1, width - cap), F32)], 1
            )
            block_ref[d] = jnp.where(below, tail, top).astype(BF)

    outs = (
        jax.ShapeDtypeStruct((peers, pad, width), BF),
        jax.ShapeDtypeStruct((1, slots), F32),
    )
    block, place = call(
        kernel,
        outs,
        10**7,
        ids,
        passages,
        in_specs=[VMEM, VMEM],
        out_specs=(VMEM, VMEM),
        name="plan",
    )
    return block, place[0].astype(jnp.int32)


def serve(wanted, bank):
    places = wanted.shape[0]
    bank_rows, width = bank.shape
    steps = 2
    cols = width // steps

    def kernel(wanted_ref, bank_ref, out, vmem, sems):
        down, along = iota((places, places), 0), iota((places, places), 1)
        want = jnp.sum(jnp.where(down == along, wanted_ref[...], 0.0), 1, keepdims=True)
        pick = (want == iota((places, bank_rows), 1).astype(F32)).astype(BF)
        copies = []
        for i in range(steps):
            at = pl.ds(i * cols, cols)
            rows = jnp.dot(pick, bank_ref[:, at], preferred_element_type=F32)
            vmem[:, at] = rows.astype(BF)
            copies.append(pltpu.make_async_copy(vmem.at[:, at], out.at[:, at], sems.at[i]))
            copies[-1].start()
        for copy in copies:
            copy.wait()

    return call(
        kernel,
        (jax.ShapeDtypeStruct((places, width), BF),),
        2 * places * bank_rows * width,
        wanted[None, :],
        bank,
        in_specs=[VMEM, VMEM],
        out_specs=(pl.BlockSpec(memory_space=pl.ANY),),
        scratch_shapes=[pltpu.VMEM((places, width), BF), pltpu.SemaphoreType.DMA((steps,))],
        compiler_params=ROOMY,
        name="serve",
    )[0]


def soften(sums, asks, counts, rows, where, pas, base=None):
    places, q_rows = asks.shape
    width = rows.shape[1]
    heads = sums.shape[0] - places // q_rows
    pad = -(-(pas + 1) // 8) * 8
    peers = heads // pad
    lines, cap = peers // 2, places // peers

    def kernel(where_ref, sums_ref, asks_ref, counts_ref, rows_ref, *refs):
        odd, source = where_ref[0] == 1, where_ref[1]
        total = 50.0 * sums_ref[...]
        asked = asks_ref[...] > 0.5
        real = iota((heads, q_rows), 0) % pad < pas
        scores = jnp.where(real, total[:heads], -jnp.inf)
        eye = iota((q_rows, q_rows), 0) == iota((q_rows, q_rows), 1)
        pos = jnp.concatenate(
            [
                jnp.sum(jnp.where(eye, total[j : j + 1], 0.0), 1, keepdims=True)
                for j in range(heads, heads + places // q_rows)
            ]
        )
        pos_or = jnp.where(asked, pos, -jnp.inf)
        top = jnp.maximum(
            jnp.max(scores, 0, keepdims=True), jnp.max(pos_or, 0, keepdims=True)
        )
        score_mass, pos_mass = jnp.exp(scores - top), jnp.exp(pos_or - top)
        mass = jnp.sum(score_mass, 0, keepdims=True) + jnp.sum(pos_mass, 0, keepdims=True)
        inv_mass = 1.0 / mass
        inv_count = 1.0 / counts_ref[...]
        weights = score_mass * inv_mass
        coeffs = jnp.where(asked, pos_mass * inv_mass - inv_count, 0.0)
        if base is None:
            losses_ref, weights_ref, hi_ref, lo_ref, sent_ref = refs
            own = jnp.sum(jnp.where(asked, pos, 0.0), 0, keepdims=True)
            losses_ref[...] = top + jnp.log(mass) - own * inv_count
            weights_ref[...] = weights.astype(BF)
            hi = coeffs.astype(BF)
            hi_ref[...] = hi
            lo_ref[...] = (coeffs - hi.astype(F32)).astype(BF)
        else:
            base_ref, sent_ref = refs
        half = lines * pad
        near_w = jnp.where(odd, weights[half:], weights[:half])
        part = jnp.dot(near_w.astype(BF), rows_ref[...], preferred_element_type=F32)
        part = part.reshape(lines, pad, width)
        coeff = jnp.sum(coeffs, 1, keepdims=True)
        if cap % 8 == 0 and 128 % cap == 0 and places % 128 == 0:
            mid = places // 2
            near_c = jnp.where(odd, coeff[mid:], coeff[:mid])
            fits = iota((mid, 128), 0) % cap == iota((mid, 128), 1) % cap
            left = jnp.where(fits, near_c, 0.0).reshape(lines, cap, 128)
            row = jnp.concatenate([jnp.sum(left, 1)] * (places // 128), 1)
            row = jnp.where(iota((lines, places), 1) // cap == source, row, 0.0)
        else:
            down, lane = iota((places, places), 0), iota((places, places), 1)
            left = jnp.where(down % cap == lane - source * cap, coeff, 0.0)
            line, at = iota((lines, places), 0), iota((lines, places), 1) // cap
            pick = (at == line + lines * where_ref[0]).astype(BF)
            row = jnp.zeros((lines, places), F32)
            for _ in range(3):
                piece = left.astype(BF)
                left = left - piece.astype(F32)
                row = row + jnp.dot(pick, piece, preferred_element_type=F32)
        if base is not None:
            part = part + base_ref[...]
            row = row + base_ref[:, pas, :places]
        sent_ref[...] = part
        for i in range(lines):
            sent_ref[i, pas : pas + 1, :places] = row[i : i + 1]

    outs = (jax.ShapeDtypeStruct((lines, pad, width), F32),)
    args = (where, sums, asks, counts, rows)
    if base is None:
        outs = (
            jax.ShapeDtypeStruct((1, q_rows), F32),
            jax.ShapeDtypeStruct((heads, q_rows), BF),
            jax.ShapeDtypeStruct((places, q_rows), BF),
            jax.ShapeDtypeStruct((places, q_rows), BF),
        ) + outs
    else:
        args += (base,)
    return call(
        kernel,
        outs,
        10**7,
        *args,
        in_specs=[pl.BlockSpec(memory_space=pltpu.SMEM)] + [VMEM] * (len(args) - 1),
        out_specs=(VMEM,) * len(outs),
        compiler_params=ROOMY,
        name="soften" if base is None else "soften_pair",
    )


def close(parts, wanted, q_got, pas, bank_rows):
    places, width = q_got.shape
    steps = 4
    cols = width // steps
    n = len(parts)

    def kernel(*refs):
        wanted_ref, q_ref, pas_out, bank_out, pas_vmem, bank_vmem, sems = refs[n:]
        total = sum(r[...] for r in refs[:n])
        pas_vmem[...] = 50.0 * total[:pas]
        copies = [pltpu.make_async_copy(pas_vmem, pas_out, sems.at[steps])]
        copies[0].start()
        back = 50.0 * total[pas : pas + 1, :places]
        row = iota((bank_rows, places), 0).astype(F32)
        member = jnp.where(row == wanted_ref[...], back, 0.0)
        hi = member.astype(BF)
        lo = (member - hi.astype(F32)).astype(BF)
        for i in range(steps):
            at = pl.ds(i * cols, cols)
            q = q_ref[:, at]
            bank_vmem[:, at] = jnp.dot(hi, q, preferred_element_type=F32) + jnp.dot(
                lo, q, preferred_element_type=F32
            )
            copies.append(
                pltpu.make_async_copy(bank_vmem.at[:, at], bank_out.at[:, at], sems.at[i])
            )
            copies[-1].start()
        for copy in copies:
            copy.wait()

    away = pl.BlockSpec(memory_space=pl.ANY)
    return call(
        kernel,
        (
            jax.ShapeDtypeStruct((pas, width), F32),
            jax.ShapeDtypeStruct((bank_rows, width), F32),
        ),
        4 * bank_rows * places * width,
        *parts,
        wanted[None, :],
        q_got,
        in_specs=[VMEM] * (n + 2),
        out_specs=(away, away),
        scratch_shapes=[
            pltpu.VMEM((pas, width), F32),
            pltpu.VMEM((bank_rows, width), F32),
            pltpu.SemaphoreType.DMA((steps + 1,)),
        ],
        compiler_params=ROOMY,
        name="close",
    )


def owns_of(counts, max_pos):
    q_rows = counts.shape[0]
    q_at = jnp.arange(q_rows)
    return jnp.concatenate(
        [
            q_at[:, None] == q_at[None, :],
            (jnp.arange(q_rows // 16 * max_pos)[:, None] // max_pos == q_at[None, :] // 16)
            & (counts[None, :] > 1),
        ]
    )


def body(queries, passages, bank, ids, counts):
    peers = lax.axis_size("dp")
    lines = peers // 2
    me = lax.axis_index("dp")
    odd = me % 2 == 1
    q_rows, width = queries.shape
    bank_rows = bank.shape[0]
    cap = bank_rows // 8
    places = peers * cap
    pas = passages.shape[0]
    pad = -(-(pas + 1) // 8) * 8
    max_pos = ids.shape[1]
    half = places // 2
    near = lambda x: jnp.where(odd, x[half:], x[:half])

    block, place = plan(ids.T, passages, peers, bank_rows, pad)
    slots = place.shape[0]
    perm = jnp.arange(places)[:, None] == place[None, :]
    heads = exchange(block, everyone())

    notes = jnp.concatenate([place.astype(BF), counts.astype(BF)])
    notes = jnp.pad(notes[None], ((0, 7), (0, width - notes.shape[0])))
    pair_in = to_pair(jnp.concatenate([queries, notes]))
    pair_q = pair_in[:q_rows]
    pair_place = pair_in[q_rows, :slots].astype(jnp.int32)
    pair_counts = pair_in[q_rows, slots : slots + q_rows].astype(jnp.int32)
    pair_perm = jnp.arange(places)[:, None] == pair_place[None, :]
    asks = dot(perm.astype(BF), owns_of(counts, max_pos).astype(BF), 1, 0)
    pair_asks = dot(pair_perm.astype(BF), owns_of(pair_counts, max_pos).astype(BF), 1, 0)
    asks, pair_asks = asks.astype(BF), pair_asks.astype(BF)

    all_pas = heads.reshape(peers * pad, width)
    wanted = heads[:, pas, :cap].astype(F32).reshape(-1)
    picked = serve(wanted, bank)
    fetched = exchange(picked.reshape(peers, cap, width), everyone()).reshape(places, width)

    send = []
    for ask, rows in ((asks, queries), (pair_asks, pair_q)):
        send.append(dot(near(ask), rows, 1, 0).astype(BF).reshape(lines, 1, cap, width))
    even_send = jnp.where(odd, send[1], send[0])
    odd_send = jnp.where(odd, send[0], send[1])
    q_send = jnp.concatenate([even_send, odd_send], 1).reshape(lines, 2 * cap, width)
    q_send, fetched = lax.optimization_barrier((q_send, fetched))
    q_got = exchange(q_send, line_groups())
    q_got = q_got.reshape(places, width)

    part = dot(all_pas, queries, 1, 1)
    pos_part = jnp.sum(jnp.where(asks > 0.5, dot(fetched, queries, 1, 1), 0.0), 1)
    mine = sub_sum(jnp.concatenate([part, pos_part.reshape(-1, q_rows)]))
    pair = to_pair(mine)
    at = 2 * place_of(line_order(lines), me // 2)
    spot = lambda source: jnp.stack([me % 2, at + source % 2]).astype(jnp.int32)
    losses, weights, hi, lo, sent = soften(
        mine, asks, counts.astype(F32)[None], queries, spot(me), pas
    )
    (sent,) = soften(
        pair, pair_asks, pair_counts.astype(F32)[None], pair_q, spot(me ^ 1), pas, sent
    )
    got = scatter_sum(sent)

    query_grad = 50.0 * (
        dot(weights, all_pas, 0, 0) + dot(hi, fetched, 0, 0) + dot(lo, fetched, 0, 0)
    )
    wanted = wanted.reshape(2, lines, cap).swapaxes(0, 1).reshape(-1)
    passage_grad, bank_grad = close(got, wanted, q_got, pas, bank_rows)
    return (losses[0], query_grad, passage_grad, bank_grad)


def solution(mesh):
    placed = (P("dp", "sub"), P("dp", "sub"), P("dp", "sub"), P("dp", None), P("dp"))
    return jax.shard_map(
        body,
        mesh=mesh,
        in_specs=placed,
        out_specs=(P("dp"), P("dp", "sub"), P("dp", "sub"), P("dp", "sub")),
        check_vma=False,
    )
```
